32 devices in a mesh: gy: 4 (over z), gx: 4 (over x, core), gz: 2 (over y).
Axes of the slice: x: 2, y: 2, z: 4, core: 2. Of those that a mesh axis runs over, the one named last changes fastest.
Arguments:
- velocity: float32 [3, 2, 768, 24, 512], P(None, None, 'gy', 'gx', 'gz'), may hold values from -6 to 6
- stencil: float32 [3, 768], replicated, may hold values from -2 to 2
- mode_rates: float32 [768], replicated, may hold values from 0.5 to 20
- basis: float32 [768, 768], P(('gx', 'gz')), may hold values from -0.21875 to 0.21875
Outputs:
- projected: float32 [3, 2, 768, 24, 512], P(None, None, 'gy', 'gx', 'gz')
The draws below stay inside these ranges and needn't reach their ends.
All inputs are finite; a program needn't handle non-finite values.
Results may differ from the reference program's by a relative error of at most 0.000075.
Values sent between devices are 32-bit elements; how exact they have to be, the bound alone decides.
No kernel may reach another device: no remote copies, remote signals or barrier semaphores. Data moves between devices by JAX's collectives and lax.ppermute only.
A program may use at most 64 MiB of HBM per device.

```python
import math
import jax
import jax.numpy as jnp
from jax import lax

NY = 768
KZ = 512
KXT = 24


def levels(key, dims, pieces, smallest, largest):
    level, own = 1.0, jax.random.fold_in(key, 6)
    for axis_at, shards_of in pieces:
        steps = jnp.exp(jax.random.uniform(jax.random.fold_in(own, axis_at), (shards_of,), jnp.float32, smallest / len(pieces), largest / len(pieces)))
        level = level * jnp.repeat(steps, dims[axis_at] // shards_of).reshape([-1 if axis == axis_at else 1 for axis in range(len(dims))])
    return level


def scatter_about(key, extent, spread, limit, shards=(), kind=jnp.bfloat16):
    factor_of = levels(key, extent, shards, -0.22, 0.18) if shards else 1.0
    array = jax.random.normal(key, extent, jnp.float32) * spread * factor_of
    return jnp.minimum(jnp.maximum(array, -limit), limit).astype(kind)


def setup_inputs(seed: int = 0) -> dict:
    key_list = jax.random.split(jax.random.key(seed), 5)
    velocity = scatter_about(key_list[0], (3, 2, NY, KXT, KZ), 1.0, 6.0, ((2, 4), (3, 4), (4, 2)), jnp.float32)
    stencil = jnp.clip(jax.random.uniform(key_list[1], (3, NY), jnp.float32, -2.0, 2.0), -2.0, 2.0)
    mode_rates = jnp.clip(jnp.exp(jax.random.uniform(key_list[2], (NY,), jnp.float32, math.log(0.5), math.log(20.0))), 0.5, 20.0)
    basis = scatter_about(key_list[3], (NY, NY), NY ** -0.5, 0.21875, ((0, 8),), jnp.float32)
    return dict(velocity=velocity, stencil=stencil, mode_rates=mode_rates, basis=basis)


def slope(field, stencil):
    padded = jnp.pad(field, ((0, 0), (1, 1), (0, 0)))
    lower = stencil[0][:, None]
    centre = stencil[1][:, None]
    upper = stencil[2][:, None]
    return lower * padded[:, :-2] + centre * field + upper * padded[:, 2:]


def reference(velocity, stencil, mode_rates, basis):
    wave_z = 0.05 * jnp.arange(KZ, dtype=jnp.int32).astype(jnp.float32)
    wave_all = 0.125 * jnp.arange(KXT, dtype=jnp.int32).astype(jnp.float32)
    moved = jnp.moveaxis(velocity, 3, 0)

    def one_mode(item):
        fields, wave_x = item
        stream = fields[0]
        normal = fields[1]
        span = fields[2]
        horizontal = jnp.stack([-(wave_x * stream[1]) - wave_z[None, :] * span[1],
                                wave_x * stream[0] + wave_z[None, :] * span[0]])
        divergence = horizontal + slope(normal, stencil)
        modal = jnp.einsum("my,ryz->rmz", basis, divergence, precision=lax.Precision.HIGHEST)
        scale = -1.0 / (mode_rates[:, None] + wave_x * wave_x + wave_z[None, :] * wave_z[None, :])
        pressure = jnp.einsum("my,rmz->ryz", basis, modal * scale[None], precision=lax.Precision.HIGHEST)
        new_stream = jnp.stack([stream[0] + wave_x * pressure[1], stream[1] - wave_x * pressure[0]])
        new_span = jnp.stack([span[0] + wave_z[None, :] * pressure[1], span[1] - wave_z[None, :] * pressure[0]])
        new_normal = normal - slope(pressure, stencil)
        return jnp.stack([new_stream, new_normal, new_span])

    result = lax.map(one_mode, (moved, wave_all))
    return jnp.moveaxis(result, 0, 3)
```

```python
import functools

import jax
import jax.numpy as jnp
from jax import lax
from jax.experimental import pallas as pl
from jax.experimental.pallas import tpu as pltpu
from jax.sharding import PartitionSpec as P


LANES = 128
EDGE = 8


def with_halo(cells, sides, width):
    for axis, dim in sides:
        count = lax.axis_size(axis)
        ends = count - 1
        head = lax.slice_in_dim(cells, 0, width, axis=dim)
        tail = lax.slice_in_dim(cells, cells.shape[dim] - width, cells.shape[dim], axis=dim)
        cells = jnp.concatenate(
            [
                lax.ppermute(tail, axis, [(i, (i + 1) % count) for i in range(ends)]),
                cells,
                lax.ppermute(head, axis, [((i + 1) % count, i) for i in range(ends)]),
            ],
            axis=dim,
        )
    return cells


def coefficients(stencil, start, count, trailing):
    rows_part = lax.dynamic_slice_in_dim(stencil, start, count, 1)
    shape = (1, count) + (1,) * trailing
    return (rows_part[0].reshape(shape), rows_part[1].reshape(shape), rows_part[2].reshape(shape))


def slope(padded, weights):
    lower, centre, upper = weights
    return lower * padded[:, :-2] + centre * padded[:, 1:-1] + upper * padded[:, 2:]


def plain_device(velocity, stencil, mode_rates, basis):
    rows_dev = velocity.shape[2]
    kx_local = velocity.shape[3]
    span_dev = velocity.shape[4]
    rows_all = stencil.shape[1]
    groups = lax.axis_size("gy")
    flat_cols = kx_local * span_dev
    pencil_cols = flat_cols // groups
    slab_index = lax.axis_index("gy")
    stream_base = lax.axis_index("gx") * kx_local
    span_base = lax.axis_index("gz") * span_dev
    wave_x = (0.125 * (stream_base + lax.iota(jnp.int32, kx_local)).astype(jnp.float32)).reshape(
        1, kx_local, 1
    )
    wave_z = (0.05 * (span_base + lax.iota(jnp.int32, span_dev)).astype(jnp.float32)).reshape(
        1, 1, span_dev
    )
    column_ids = slab_index * pencil_cols + lax.iota(jnp.int32, pencil_cols)
    wave_px = 0.125 * (stream_base + column_ids // span_dev).astype(jnp.float32)
    wave_pz = 0.05 * (span_base + column_ids % span_dev).astype(jnp.float32)
    local_weights = coefficients(stencil, slab_index * rows_dev, rows_dev, 2)
    full_basis = lax.all_gather(basis, ("gx", "gz"), axis=0, tiled=True)
    stream = velocity[0]
    normal = velocity[1]
    span = velocity[2]
    horizontal = jnp.stack(
        [-(wave_x * stream[1]) - wave_z * span[1], wave_x * stream[0] + wave_z * span[0]]
    )
    padded = with_halo(normal, (("gy", 1),), 1)
    divergence = (horizontal + slope(padded, local_weights)).reshape(2, rows_dev, flat_cols)
    columns = lax.all_to_all(divergence, "gy", split_axis=2, concat_axis=1, tiled=True)
    modal = jnp.einsum("my,ryp->rmp", full_basis, columns, precision=lax.Precision.HIGHEST)
    scale = -1.0 / (
        mode_rates.reshape(rows_all, 1)
        + (wave_px * wave_px + wave_pz * wave_pz).reshape(1, pencil_cols)
    )
    pressure = jnp.einsum(
        "my,rmp->ryp", full_basis, modal * scale[None], precision=lax.Precision.HIGHEST
    )
    press_flat = lax.all_to_all(pressure, "gy", split_axis=1, concat_axis=2, tiled=True)
    press_slab = press_flat.reshape(2, rows_dev, kx_local, span_dev)
    press_padded = with_halo(press_slab, (("gy", 1),), 1)
    press_slope = slope(press_padded, local_weights)
    new_stream = jnp.stack([stream[0] + wave_x * press_slab[1], stream[1] - wave_x * press_slab[0]])
    new_span = jnp.stack([span[0] + wave_z * press_slab[1], span[1] - wave_z * press_slab[0]])
    new_normal = normal - press_slope
    return jnp.stack([new_stream, new_normal, new_span])


def unit_waves(place, unit, halves, gap):
    kx = lax.div(unit, halves)
    half = lax.rem(unit, halves)
    wave_x = 0.125 * (place[1] + kx).astype(jnp.float32)
    lane = lax.broadcasted_iota(jnp.int32, (gap, LANES), 1)
    wave_z = 0.05 * (place[2] + half * LANES + lane).astype(jnp.float32)
    return wave_x, wave_z


def shifted(field, before, after):
    rows = field.shape[0]
    row = lax.broadcasted_iota(jnp.int32, field.shape, 0)
    prev = jnp.where(row == 0, before, pltpu.roll(field, 1, 0))
    nxt = jnp.where(row == rows - 1, after, pltpu.roll(field, rows - 1, 0))
    return prev, nxt


def divergence_kernel(chunk, groups, halves, place, vel, weights, *outs):
    step = pl.program_id(0)
    rows = vel.shape[3]
    unit = chunk * groups + lax.rem(place[0] + step, groups)
    wave_x, wave_z = unit_waves(place, unit, halves, 1)

    def write(out):
        edges = []
        for part, sign in ((0, -1.0), (1, 1.0)):
            normal = vel[1, part, 0]
            prev, nxt = shifted(normal, 0.0, 0.0)
            out[part * rows : (part + 1) * rows, :] = (
                sign * (wave_x * vel[0, 1 - part, 0] + wave_z * vel[2, 1 - part, 0])
                + (weights[0] * prev + weights[1] * normal + weights[2] * nxt)
            )
            edges += [vel[1, part, 0, 0:1, :], vel[1, part, 0, rows - 1 : rows, :]]
        edges.append(jnp.zeros((EDGE - 4, LANES), jnp.float32))
        out[2 * rows :, :] = jnp.concatenate(edges, 0)

    for k in range(groups):
        pl.when(step == k)(functools.partial(write, outs[k]))


def split_kernel(pieces, *refs):
    sources, (high, low, high_t, low_t), full = refs[:pieces], refs[pieces:-1], refs[-1]
    at = 0
    for source in sources:
        full[at : at + source.shape[0], :] = source[...]
        at += source.shape[0]
    size = full.shape[0]
    for j in range(0, size, LANES):
        block = full[j : j + LANES, :]
        top = block.astype(jnp.bfloat16)
        high[j : j + LANES, :] = top
        low[j : j + LANES, :] = (block - top.astype(jnp.float32)).astype(jnp.bfloat16)
        block = full[:, j : j + LANES].T
        top = block.astype(jnp.bfloat16)
        high_t[j : j + LANES, :] = top
        low_t[j : j + LANES, :] = (block - top.astype(jnp.float32)).astype(jnp.bfloat16)


def three_products(high, low, values):
    top = values.astype(jnp.bfloat16)
    rest = (values - top.astype(jnp.float32)).astype(jnp.bfloat16)
    dot = functools.partial(jnp.dot, preferred_element_type=jnp.float32)
    return dot(high[...], top) + (dot(high[...], rest) + dot(low[...], top))


def solve_kernel(chunk, groups, halves, place, stencil, rates, high, low, high_t, low_t, *refs):
    blocks, outs = refs[:groups], refs[groups : 2 * groups]
    field, edge = refs[2 * groups :]
    rows = (blocks[0].shape[0] - EDGE) // 2
    rows_all = high.shape[0]
    me = place[0]
    for k in range(groups):
        source = lax.rem(me - k + groups, groups)
        base = pl.multiple_of(source * rows + EDGE, EDGE)
        for part in range(2):
            field[pl.ds(base, rows), part * LANES : (part + 1) * LANES] = blocks[k][
                part * rows : (part + 1) * rows, :
            ]
        edge[source] = blocks[k][2 * rows :, :]
    for s in range(groups - 1):
        cut = (s + 1) * rows
        for part in range(2):
            lanes = slice(part * LANES, (part + 1) * LANES)
            above = edge[s + 1, 2 * part : 2 * part + 1, :]
            below = edge[s, 2 * part + 1 : 2 * part + 2, :]
            field[EDGE + cut - 1 : EDGE + cut, lanes] += stencil[2, cut - 1] * above
            field[EDGE + cut : EDGE + cut + 1, lanes] += stencil[0, cut] * below
    modal = three_products(high, low, field[EDGE : EDGE + rows_all, :])
    wave_x, wave_z = unit_waves(place, chunk * groups + me, halves, 1)
    scale = -1.0 / (rates[...] + wave_x * wave_x + wave_z * wave_z)
    modal = jnp.concatenate([modal[:, :LANES] * scale, modal[:, LANES:] * scale], 1)
    field[EDGE : EDGE + rows_all, :] = three_products(high_t, low_t, modal)
    field[0:EDGE, :] = jnp.zeros((EDGE, 2 * LANES), jnp.float32)
    field[EDGE + rows_all :, :] = jnp.zeros((EDGE, 2 * LANES), jnp.float32)
    for k in range(groups):
        target = lax.rem(me + k, groups)
        start = pl.multiple_of(target * rows, EDGE)
        edges = []
        for part in range(2):
            lanes = slice(part * LANES, (part + 1) * LANES)
            outs[k][part * rows : (part + 1) * rows, :] = field[pl.ds(start + EDGE, rows), lanes]
            edges.append(field[pl.ds(start, EDGE), lanes][EDGE - 1 :, :])
            edges.append(field[pl.ds(start + EDGE + rows, EDGE), lanes][:1, :])
        edges.append(jnp.zeros((EDGE - 4, LANES), jnp.float32))
        outs[k][2 * rows :, :] = jnp.concatenate(edges, 0)


def project_kernel(chunk, groups, halves, place, vel, weights, *refs):
    blocks, out = refs[:groups], refs[-1]
    step = pl.program_id(0)
    rows = vel.shape[3]
    unit = chunk * groups + lax.rem(place[0] - step + groups, groups)
    wave_x, wave_z = unit_waves(place, unit, halves, 1)

    def write(block):
        for part, sign in ((0, 1.0), (1, -1.0)):
            other = block[(1 - part) * rows : (2 - part) * rows, :]
            out[0, part, 0] = vel[0, part, 0] + (sign * wave_x) * other
            out[2, part, 0] = vel[2, part, 0] + (sign * wave_z) * other
            press = block[part * rows : (part + 1) * rows, :]
            at = 2 * rows + 2 * part
            prev, nxt = shifted(press, block[at : at + 1, :], block[at + 1 : at + 2, :])
            out[1, part, 0] = vel[1, part, 0] - (
                weights[0] * prev + weights[1] * press + weights[2] * nxt
            )

    for k in range(groups):
        pl.when(step == k)(functools.partial(write, blocks[k]))


def gathered_rows(basis, mode_rates):
    gx, gz = lax.axis_size("gx"), lax.axis_size("gz")
    names = ("gx", "gz")
    if (gx, gz) != (4, 2):
        return [lax.all_gather(basis, names, axis=0, tiled=True)], mode_rates
    swap = lambda value, a, b: lax.ppermute(
        value,
        names,
        [(x * gz + z, (x ^ a) * gz + (z ^ b)) for x in range(gx) for z in range(gz)],
    )
    flips = ((0, 0), (2, 0), (0, 1), (2, 1))
    pieces = [basis] + [swap(basis, a, b) for a, b in flips[1:]]
    pieces += [swap(piece, 1, 0) for piece in pieces]
    count = basis.shape[0]
    x, z = lax.axis_index("gx"), lax.axis_index("gz")
    order = [(a + c, b) for c in (0, 1) for a, b in flips]
    rates = jnp.concatenate(
        [
            lax.dynamic_slice_in_dim(mode_rates, ((x ^ a) * gz + (z ^ b)) * count, count, 0)
            for a, b in order
        ]
    )
    return pieces, rates


def fast_device(velocity, stencil, mode_rates, basis):
    rows, kx_local, span_dev = velocity.shape[2:]
    rows_all = stencil.shape[1]
    groups = lax.axis_size("gy")
    halves = span_dev // LANES
    chunks = kx_local * halves // groups
    me = lax.axis_index("gy")
    place = jnp.stack(
        [me, lax.axis_index("gx") * kx_local, lax.axis_index("gz") * span_dev]
    ).astype(jnp.int32)
    vel = jnp.transpose(velocity, (0, 1, 3, 2, 4))
    weights = jnp.broadcast_to(
        lax.dynamic_slice_in_dim(stencil, me * rows, rows, 1)[:, :, None], (3, rows, LANES)
    )
    block = jax.ShapeDtypeStruct((2 * rows + EDGE, LANES), jnp.float32)
    whole = pl.BlockSpec(memory_space=pltpu.VMEM)
    held = pl.BlockSpec(block.shape, lambda i, s: (0, 0))
    held_weights = pl.BlockSpec(weights.shape, lambda i, s: (0, 0, 0))
    unit_bytes = 6 * rows * LANES * 4
    params = pltpu.CompilerParams(vmem_limit_bytes=40 * 2**20)

    def unit_spec(chunk, sign):
        def index(i, s):
            unit = chunk * groups + lax.rem(s[0] + sign * i + groups, groups)
            return 0, 0, lax.div(unit, halves), 0, lax.rem(unit, halves)

        return pl.BlockSpec((3, 2, 1, rows, LANES), index)

    def exchange(parts):
        return [parts[0]] + [
            lax.ppermute(parts[k], "gy", [(s, (s + k) % groups) for s in range(groups)])
            for k in range(1, groups)
        ]

    def diverge(chunk):
        return pl.pallas_call(
            functools.partial(divergence_kernel, chunk, groups, halves),
            grid_spec=pltpu.PrefetchScalarGridSpec(
                num_scalar_prefetch=1,
                grid=(groups,),
                in_specs=[unit_spec(chunk, 1), held_weights],
                out_specs=[held] * groups,
            ),
            out_shape=[block] * groups,
            compiler_params=params,
            name="divergence",
            cost_estimate=pl.CostEstimate(
                flops=groups * unit_bytes, bytes_accessed=2 * groups * unit_bytes, transcendentals=0
            ),
        )(place, vel, weights)

    arrived = [exchange(diverge(chunk)) for chunk in range(chunks)]
    pieces, rates = gathered_rows(basis, mode_rates)
    rates = jnp.broadcast_to(rates[:, None], (rows_all, LANES))
    matrix = jax.ShapeDtypeStruct((rows_all, rows_all), jnp.bfloat16)
    splits = pl.pallas_call(
        functools.partial(split_kernel, len(pieces)),
        in_specs=[whole] * len(pieces),
        out_specs=[whole] * 4,
        out_shape=[matrix] * 4,
        scratch_shapes=[pltpu.VMEM((rows_all, rows_all), jnp.float32)],
        compiler_params=params,
        name="split",
        cost_estimate=pl.CostEstimate(
            flops=4 * rows_all**2, bytes_accessed=12 * rows_all**2, transcendentals=0
        ),
    )(*pieces)

    def solve(chunk, blocks):
        return pl.pallas_call(
            functools.partial(solve_kernel, chunk, groups, halves),
            in_specs=[pl.BlockSpec(memory_space=pltpu.SMEM)] * 2 + [whole] * (5 + groups),
            out_specs=[whole] * groups,
            out_shape=[block] * groups,
            scratch_shapes=[
                pltpu.VMEM((rows_all + 2 * EDGE, 2 * LANES), jnp.float32),
                pltpu.VMEM((groups, EDGE, LANES), jnp.float32),
            ],
            compiler_params=params,
            name="solve",
            cost_estimate=pl.CostEstimate(
                flops=12 * rows_all**2 * 2 * LANES,
                bytes_accessed=8 * rows_all**2 + 8 * block.size * groups,
                transcendentals=0,
            ),
        )(place, stencil, rates, *splits, *blocks)

    returned = [exchange(solve(chunk, arrived[chunk])) for chunk in range(chunks)]
    out = None
    for chunk in range(chunks):
        carried = [] if out is None else [out]
        out = pl.pallas_call(
            functools.partial(project_kernel, chunk, groups, halves),
            grid_spec=pltpu.PrefetchScalarGridSpec(
                num_scalar_prefetch=1,
                grid=(groups,),
                in_specs=[unit_spec(chunk, -1), held_weights]
                + [held] * groups
                + [pl.BlockSpec(memory_space=pl.ANY)] * len(carried),
                out_specs=unit_spec(chunk, -1),
            ),
            out_shape=jax.ShapeDtypeStruct(vel.shape, jnp.float32),
            input_output_aliases={3 + groups: 0} if carried else {},
            compiler_params=params,
            name="project",
            cost_estimate=pl.CostEstimate(
                flops=groups * unit_bytes, bytes_accessed=3 * groups * unit_bytes, transcendentals=0
            ),
        )(place, vel, weights, *returned[chunk], *carried)
    return jnp.transpose(out, (0, 1, 3, 2, 4))


def per_device(velocity, stencil, mode_rates, basis):
    rows, kx_local, span_dev = velocity.shape[2:]
    groups = lax.axis_size("gy")
    units = kx_local * (span_dev // LANES)
    fits = (
        span_dev % LANES == 0
        and units >= groups
        and units % groups == 0
        and rows % EDGE == 0
        and stencil.shape[1] % LANES == 0
        and basis.shape[0] % EDGE == 0
    )
    return (fast_device if fits else plain_device)(velocity, stencil, mode_rates, basis)


def solution(mesh):
    placed = (P(None, None, "gy", "gx", "gz"), P(), P(), P(("gx", "gz"), None))
    return jax.shard_map(
        per_device,
        mesh=mesh,
        in_specs=placed,
        out_specs=P(None, None, "gy", "gx", "gz"),
        check_vma=False,
    )
```

```python
import functools

import jax
import jax.numpy as jnp
from jax import lax
from jax.experimental import pallas as pl
from jax.experimental.pallas import tpu as pltpu
from jax.sharding import PartitionSpec as P


LANES = 128
EDGE = 8


def with_halo(cells, sides, width):
    for axis, dim in sides:
        count = lax.axis_size(axis)
        ends = count - 1
        head = lax.slice_in_dim(cells, 0, width, axis=dim)
        tail = lax.slice_in_dim(cells, cells.shape[dim] - width, cells.shape[dim], axis=dim)
        cells = jnp.concatenate(
            [
                lax.ppermute(tail, axis, [(i, (i + 1) % count) for i in range(ends)]),
                cells,
                lax.ppermute(head, axis, [((i + 1) % count, i) for i in range(ends)]),
            ],
            axis=dim,
        )
    return cells


def coefficients(stencil, start, count, trailing):
    rows_part = lax.dynamic_slice_in_dim(stencil, start, count, 1)
    shape = (1, count) + (1,) * trailing
    return (rows_part[0].reshape(shape), rows_part[1].reshape(shape), rows_part[2].reshape(shape))


def slope(padded, weights):
    lower, centre, upper = weights
    return lower * padded[:, :-2] + centre * padded[:, 1:-1] + upper * padded[:, 2:]


def plain_device(velocity, stencil, mode_rates, basis):
    rows_dev = velocity.shape[2]
    kx_local = velocity.shape[3]
    span_dev = velocity.shape[4]
    rows_all = stencil.shape[1]
    groups = lax.axis_size("gy")
    flat_cols = kx_local * span_dev
    pencil_cols = flat_cols // groups
    slab_index = lax.axis_index("gy")
    stream_base = lax.axis_index("gx") * kx_local
    span_base = lax.axis_index("gz") * span_dev
    wave_x = (0.125 * (stream_base + lax.iota(jnp.int32, kx_local)).astype(jnp.float32)).reshape(
        1, kx_local, 1
    )
    wave_z = (0.05 * (span_base + lax.iota(jnp.int32, span_dev)).astype(jnp.float32)).reshape(
        1, 1, span_dev
    )
    column_ids = slab_index * pencil_cols + lax.iota(jnp.int32, pencil_cols)
    wave_px = 0.125 * (stream_base + column_ids // span_dev).astype(jnp.float32)
    wave_pz = 0.05 * (span_base + column_ids % span_dev).astype(jnp.float32)
    local_weights = coefficients(stencil, slab_index * rows_dev, rows_dev, 2)
    full_basis = lax.all_gather(basis, ("gx", "gz"), axis=0, tiled=True)
    stream = velocity[0]
    normal = velocity[1]
    span = velocity[2]
    horizontal = jnp.stack(
        [-(wave_x * stream[1]) - wave_z * span[1], wave_x * stream[0] + wave_z * span[0]]
    )
    padded = with_halo(normal, (("gy", 1),), 1)
    divergence = (horizontal + slope(padded, local_weights)).reshape(2, rows_dev, flat_cols)
    columns = lax.all_to_all(divergence, "gy", split_axis=2, concat_axis=1, tiled=True)
    modal = jnp.einsum("my,ryp->rmp", full_basis, columns, precision=lax.Precision.HIGHEST)
    scale = -1.0 / (
        mode_rates.reshape(rows_all, 1)
        + (wave_px * wave_px + wave_pz * wave_pz).reshape(1, pencil_cols)
    )
    pressure = jnp.einsum(
        "my,rmp->ryp", full_basis, modal * scale[None], precision=lax.Precision.HIGHEST
    )
    press_flat = lax.all_to_all(pressure, "gy", split_axis=1, concat_axis=2, tiled=True)
    press_slab = press_flat.reshape(2, rows_dev, kx_local, span_dev)
    press_padded = with_halo(press_slab, (("gy", 1),), 1)
    press_slope = slope(press_padded, local_weights)
    new_stream = jnp.stack([stream[0] + wave_x * press_slab[1], stream[1] - wave_x * press_slab[0]])
    new_span = jnp.stack([span[0] + wave_z * press_slab[1], span[1] - wave_z * press_slab[0]])
    new_normal = normal - press_slope
    return jnp.stack([new_stream, new_normal, new_span])


def unit_waves(place, unit, halves, gap):
    kx = lax.div(unit, halves)
    half = lax.rem(unit, halves)
    wave_x = 0.125 * (place[1] + kx).astype(jnp.float32)
    lane = lax.broadcasted_iota(jnp.int32, (gap, LANES), 1)
    wave_z = 0.05 * (place[2] + half * LANES + lane).astype(jnp.float32)
    return wave_x, wave_z


def shifted(field, before, after):
    rows = field.shape[0]
    row = lax.broadcasted_iota(jnp.int32, field.shape, 0)
    prev = jnp.where(row == 0, before, pltpu.roll(field, 1, 0))
    nxt = jnp.where(row == rows - 1, after, pltpu.roll(field, rows - 1, 0))
    return prev, nxt


def divergence_kernel(chunk, groups, halves, place, vel, weights, *outs):
    step = pl.program_id(0)
    rows = vel.shape[3]
    unit = chunk * groups + lax.rem(place[0] + step, groups)
    wave_x, wave_z = unit_waves(place, unit, halves, 1)

    def write(out):
        edges = []
        for part, sign in ((0, -1.0), (1, 1.0)):
            normal = vel[1, part, 0]
            prev, nxt = shifted(normal, 0.0, 0.0)
            out[part * rows : (part + 1) * rows, :] = (
                sign * (wave_x * vel[0, 1 - part, 0] + wave_z * vel[2, 1 - part, 0])
                + (weights[0] * prev + weights[1] * normal + weights[2] * nxt)
            )
            edges += [vel[1, part, 0, 0:1, :], vel[1, part, 0, rows - 1 : rows, :]]
        edges.append(jnp.zeros((EDGE - 4, LANES), jnp.float32))
        out[2 * rows :, :] = jnp.concatenate(edges, 0)

    for k in range(groups):
        pl.when(step == k)(functools.partial(write, outs[k]))


def split_kernel(pieces, *refs):
    sources, (high, low, high_t, low_t), full = refs[:pieces], refs[pieces:-1], refs[-1]
    at = 0
    for source in sources:
        full[at : at + source.shape[0], :] = source[...]
        at += source.shape[0]
    size = full.shape[0]
    for j in range(0, size, LANES):
        block = full[j : j + LANES, :]
        top = block.astype(jnp.bfloat16)
        high[j : j + LANES, :] = top
        low[j : j + LANES, :] = (block - top.astype(jnp.float32)).astype(jnp.bfloat16)
        block = full[:, j : j + LANES].T
        top = block.astype(jnp.bfloat16)
        high_t[j : j + LANES, :] = top
        low_t[j : j + LANES, :] = (block - top.astype(jnp.float32)).astype(jnp.bfloat16)


def three_products(high, low, values):
    top = values.astype(jnp.bfloat16)
    rest = (values - top.astype(jnp.float32)).astype(jnp.bfloat16)
    dot = functools.partial(jnp.dot, preferred_element_type=jnp.float32)
    return dot(high[...], top) + (dot(high[...], rest) + dot(low[...], top))


def solve_kernel(chunk, groups, halves, place, stencil, rates, high, low, high_t, low_t, *refs):
    blocks, outs = refs[:groups], refs[groups : 2 * groups]
    field, edge = refs[2 * groups :]
    rows = (blocks[0].shape[0] - EDGE) // 2
    rows_all = high.shape[0]
    me = place[0]
    for k in range(groups):
        source = lax.rem(me - k + groups, groups)
        base = pl.multiple_of(source * rows + EDGE, EDGE)
        for part in range(2):
            field[pl.ds(base, rows), part * LANES : (part + 1) * LANES] = blocks[k][
                part * rows : (part + 1) * rows, :
            ]
        edge[source] = blocks[k][2 * rows :, :]
    for s in range(groups - 1):
        cut = (s + 1) * rows
        for part in range(2):
            lanes = slice(part * LANES, (part + 1) * LANES)
            above = edge[s + 1, 2 * part : 2 * part + 1, :]
            below = edge[s, 2 * part + 1 : 2 * part + 2, :]
            field[EDGE + cut - 1 : EDGE + cut, lanes] += stencil[2, cut - 1] * above
            field[EDGE + cut : EDGE + cut + 1, lanes] += stencil[0, cut] * below
    modal = three_products(high, low, field[EDGE : EDGE + rows_all, :])
    wave_x, wave_z = unit_waves(place, chunk * groups + me, halves, 1)
    scale = -1.0 / (rates[...] + wave_x * wave_x + wave_z * wave_z)
    modal = jnp.concatenate([modal[:, :LANES] * scale, modal[:, LANES:] * scale], 1)
    field[EDGE : EDGE + rows_all, :] = three_products(high_t, low_t, modal)
    field[0:EDGE, :] = jnp.zeros((EDGE, 2 * LANES), jnp.float32)
    field[EDGE + rows_all :, :] = jnp.zeros((EDGE, 2 * LANES), jnp.float32)
    for k in range(groups):
        target = lax.rem(me + k, groups)
        start = pl.multiple_of(target * rows, EDGE)
        edges = []
        for part in range(2):
            lanes = slice(part * LANES, (part + 1) * LANES)
            outs[k][part * rows : (part + 1) * rows, :] = field[pl.ds(start + EDGE, rows), lanes]
            edges.append(field[pl.ds(start, EDGE), lanes][EDGE - 1 :, :])
            edges.append(field[pl.ds(start + EDGE + rows, EDGE), lanes][:1, :])
        edges.append(jnp.zeros((EDGE - 4, LANES), jnp.float32))
        outs[k][2 * rows :, :] = jnp.concatenate(edges, 0)


def project_kernel(chunk, groups, halves, place, vel, weights, *refs):
    blocks, out = refs[:groups], refs[-1]
    step = pl.program_id(0)
    rows = vel.shape[3]
    unit = chunk * groups + lax.rem(place[0] - step + groups, groups)
    wave_x, wave_z = unit_waves(place, unit, halves, 1)

    def write(block):
        for part, sign in ((0, 1.0), (1, -1.0)):
            other = block[(1 - part) * rows : (2 - part) * rows, :]
            out[0, part, 0] = vel[0, part, 0] + (sign * wave_x) * other
            out[2, part, 0] = vel[2, part, 0] + (sign * wave_z) * other
            press = block[part * rows : (part + 1) * rows, :]
            at = 2 * rows + 2 * part
            prev, nxt = shifted(press, block[at : at + 1, :], block[at + 1 : at + 2, :])
            out[1, part, 0] = vel[1, part, 0] - (
                weights[0] * prev + weights[1] * press + weights[2] * nxt
            )

    for k in range(groups):
        pl.when(step == k)(functools.partial(write, blocks[k]))


def shift_order(groups):
    return sorted(range(1, groups), key=lambda k: abs(2 * k - groups))


def gathered_rows(basis, mode_rates):
    gx, gz = lax.axis_size("gx"), lax.axis_size("gz")
    names = ("gx", "gz")
    if (gx, gz) != (4, 2):
        return [lax.all_gather(basis, names, axis=0, tiled=True)], mode_rates

    def swap(value, a, b):
        return lax.ppermute(
            value,
            names,
            [(x * gz + z, (x ^ a) * gz + (z ^ b)) for x in range(gx) for z in range(gz)],
        )

    flips = ((0, 0), (2, 0), (0, 1), (2, 1))
    pieces = [basis] + [swap(basis, *flips[i]) for i in range(1, 4)]
    pieces += [swap(piece, 1, 0) for piece in pieces]
    count = basis.shape[0]
    x, z = lax.axis_index("gx"), lax.axis_index("gz")
    order = [(a + c, b) for c in (0, 1) for a, b in flips]
    rates = jnp.concatenate(
        [
            lax.dynamic_slice_in_dim(mode_rates, ((x ^ a) * gz + (z ^ b)) * count, count, 0)
            for a, b in order
        ]
    )
    return pieces, rates


def fast_device(velocity, stencil, mode_rates, basis):
    rows, kx_local, span_dev = velocity.shape[2:]
    rows_all = stencil.shape[1]
    groups = lax.axis_size("gy")
    halves = span_dev // LANES
    chunks = kx_local * halves // groups
    me = lax.axis_index("gy")
    place = jnp.stack(
        [me, lax.axis_index("gx") * kx_local, lax.axis_index("gz") * span_dev]
    ).astype(jnp.int32)
    vel = jnp.transpose(velocity, (0, 1, 3, 2, 4))
    weights = jnp.broadcast_to(
        lax.dynamic_slice_in_dim(stencil, me * rows, rows, 1)[:, :, None], (3, rows, LANES)
    )
    block = jax.ShapeDtypeStruct((2 * rows + EDGE, LANES), jnp.float32)
    whole = pl.BlockSpec(memory_space=pltpu.VMEM)
    held = pl.BlockSpec(block.shape, lambda i, s: (0, 0))
    held_weights = pl.BlockSpec(weights.shape, lambda i, s: (0, 0, 0))
    unit_bytes = 6 * rows * LANES * 4
    params = pltpu.CompilerParams(vmem_limit_bytes=40 * 2**20)
    wide_params = pltpu.CompilerParams(vmem_limit_bytes=60 * 2**20)

    def unit_spec(chunk, sign):
        def index(i, s):
            unit = chunk * groups + lax.rem(s[0] + sign * i + groups, groups)
            return 0, 0, lax.div(unit, halves), 0, lax.rem(unit, halves)

        return pl.BlockSpec((3, 2, 1, rows, LANES), index)

    def exchange(parts):
        sent = {0: parts[0]}
        for k in shift_order(groups):
            sent[k] = lax.ppermute(parts[k], "gy", [(s, (s + k) % groups) for s in range(groups)])
        return [sent[k] for k in range(groups)]

    def diverge(chunk):
        return pl.pallas_call(
            functools.partial(divergence_kernel, chunk, groups, halves),
            grid_spec=pltpu.PrefetchScalarGridSpec(
                num_scalar_prefetch=1,
                grid=(groups,),
                in_specs=[unit_spec(chunk, 1), held_weights],
                out_specs=[held] * groups,
            ),
            out_shape=[block] * groups,
            compiler_params=wide_params,
            name="divergence",
            cost_estimate=pl.CostEstimate(
                flops=groups * unit_bytes, bytes_accessed=2 * groups * unit_bytes, transcendentals=0
            ),
        )(place, vel, weights)

    arrived = []
    for chunk in range(chunks):
        parts = diverge(chunk)
        arrived.append(exchange(parts))
    pieces, rates = gathered_rows(basis, mode_rates)
    rates = jnp.broadcast_to(rates[:, None], (rows_all, LANES))
    matrix = jax.ShapeDtypeStruct((rows_all, rows_all), jnp.bfloat16)
    splits = pl.pallas_call(
        functools.partial(split_kernel, len(pieces)),
        in_specs=[whole] * len(pieces),
        out_specs=[whole] * 4,
        out_shape=[matrix] * 4,
        scratch_shapes=[pltpu.VMEM((rows_all, rows_all), jnp.float32)],
        compiler_params=params,
        name="split",
        cost_estimate=pl.CostEstimate(
            flops=4 * rows_all**2, bytes_accessed=12 * rows_all**2, transcendentals=0
        ),
    )(*pieces)

    def solve(chunk, blocks):
        return pl.pallas_call(
            functools.partial(solve_kernel, chunk, groups, halves),
            in_specs=[pl.BlockSpec(memory_space=pltpu.SMEM)] * 2 + [whole] * (5 + groups),
            out_specs=[whole] * groups,
            out_shape=[block] * groups,
            scratch_shapes=[
                pltpu.VMEM((rows_all + 2 * EDGE, 2 * LANES), jnp.float32),
                pltpu.VMEM((groups, EDGE, LANES), jnp.float32),
            ],
            compiler_params=params,
            name="solve",
            cost_estimate=pl.CostEstimate(
                flops=12 * rows_all**2 * 2 * LANES,
                bytes_accessed=8 * rows_all**2 + 8 * block.size * groups,
                transcendentals=0,
            ),
        )(place, stencil, rates, *splits, *blocks)

    returned = []
    for chunk in range(chunks):
        parts = solve(chunk, arrived[chunk])
        returned.append(exchange(parts))
    out = None
    for chunk in range(chunks):
        carried = [] if out is None else [out]
        call = pl.pallas_call(
            functools.partial(project_kernel, chunk, groups, halves),
            grid_spec=pltpu.PrefetchScalarGridSpec(
                num_scalar_prefetch=1,
                grid=(groups,),
                in_specs=[unit_spec(chunk, -1), held_weights]
                + [held] * groups
                + [pl.BlockSpec(memory_space=pl.ANY)] * len(carried),
                out_specs=unit_spec(chunk, -1),
            ),
            out_shape=jax.ShapeDtypeStruct(vel.shape, jnp.float32),
            input_output_aliases={3 + groups: 0} if carried else {},
            compiler_params=params,
            name="project",
            cost_estimate=pl.CostEstimate(
                flops=groups * unit_bytes, bytes_accessed=3 * groups * unit_bytes, transcendentals=0
            ),
        )
        out = call(place, vel, weights, *returned[chunk], *carried)
    return jnp.transpose(out, (0, 1, 3, 2, 4))


def fits(shape, rows_all, groups):
    rows, kx_local, span_dev = shape
    units = kx_local * (span_dev // LANES)
    return (
        span_dev % LANES == 0
        and units >= groups
        and units % groups == 0
        and rows % EDGE == 0
        and rows_all % LANES == 0
    )


def per_device(velocity, stencil, mode_rates, basis):
    if not fits(velocity.shape[2:], stencil.shape[1], lax.axis_size("gy")):
        return plain_device(velocity, stencil, mode_rates, basis)
    return fast_device(velocity, stencil, mode_rates, basis)


def solution(mesh):
    placed = (P(None, None, "gy", "gx", "gz"), P(), P(), P(("gx", "gz"), None))
    return jax.shard_map(
        per_device,
        mesh=mesh,
        in_specs=placed,
        out_specs=P(None, None, "gy", "gx", "gz"),
        check_vma=False,
    )
```

```python
import functools

import jax
import jax.numpy as jnp
from jax import lax
from jax.experimental import pallas as pl
from jax.experimental.pallas import tpu as pltpu
from jax.sharding import PartitionSpec as P


LANES = 128
EDGE = 8


def with_halo(cells, sides, width):
    for axis, dim in sides:
        count = lax.axis_size(axis)
        ends = count - 1
        head = lax.slice_in_dim(cells, 0, width, axis=dim)
        tail = lax.slice_in_dim(cells, cells.shape[dim] - width, cells.shape[dim], axis=dim)
        cells = jnp.concatenate(
            [
                lax.ppermute(tail, axis, [(i, (i + 1) % count) for i in range(ends)]),
                cells,
                lax.ppermute(head, axis, [((i + 1) % count, i) for i in range(ends)]),
            ],
            axis=dim,
        )
    return cells


def coefficients(stencil, start, count, trailing):
    rows_part = lax.dynamic_slice_in_dim(stencil, start, count, 1)
    shape = (1, count) + (1,) * trailing
    return (rows_part[0].reshape(shape), rows_part[1].reshape(shape), rows_part[2].reshape(shape))


def slope(padded, weights):
    lower, centre, upper = weights
    return lower * padded[:, :-2] + centre * padded[:, 1:-1] + upper * padded[:, 2:]


def plain_device(velocity, stencil, mode_rates, basis):
    rows_dev = velocity.shape[2]
    kx_local = velocity.shape[3]
    span_dev = velocity.shape[4]
    rows_all = stencil.shape[1]
    groups = lax.axis_size("gy")
    flat_cols = kx_local * span_dev
    pencil_cols = flat_cols // groups
    slab_index = lax.axis_index("gy")
    stream_base = lax.axis_index("gx") * kx_local
    span_base = lax.axis_index("gz") * span_dev
    wave_x = (0.125 * (stream_base + lax.iota(jnp.int32, kx_local)).astype(jnp.float32)).reshape(
        1, kx_local, 1
    )
    wave_z = (0.05 * (span_base + lax.iota(jnp.int32, span_dev)).astype(jnp.float32)).reshape(
        1, 1, span_dev
    )
    column_ids = slab_index * pencil_cols + lax.iota(jnp.int32, pencil_cols)
    wave_px = 0.125 * (stream_base + column_ids // span_dev).astype(jnp.float32)
    wave_pz = 0.05 * (span_base + column_ids % span_dev).astype(jnp.float32)
    local_weights = coefficients(stencil, slab_index * rows_dev, rows_dev, 2)
    full_basis = lax.all_gather(basis, ("gx", "gz"), axis=0, tiled=True)
    stream = velocity[0]
    normal = velocity[1]
    span = velocity[2]
    horizontal = jnp.stack(
        [-(wave_x * stream[1]) - wave_z * span[1], wave_x * stream[0] + wave_z * span[0]]
    )
    padded = with_halo(normal, (("gy", 1),), 1)
    divergence = (horizontal + slope(padded, local_weights)).reshape(2, rows_dev, flat_cols)
    columns = lax.all_to_all(divergence, "gy", split_axis=2, concat_axis=1, tiled=True)
    modal = jnp.einsum("my,ryp->rmp", full_basis, columns, precision=lax.Precision.HIGHEST)
    scale = -1.0 / (
        mode_rates.reshape(rows_all, 1)
        + (wave_px * wave_px + wave_pz * wave_pz).reshape(1, pencil_cols)
    )
    pressure = jnp.einsum(
        "my,rmp->ryp", full_basis, modal * scale[None], precision=lax.Precision.HIGHEST
    )
    press_flat = lax.all_to_all(pressure, "gy", split_axis=1, concat_axis=2, tiled=True)
    press_slab = press_flat.reshape(2, rows_dev, kx_local, span_dev)
    press_padded = with_halo(press_slab, (("gy", 1),), 1)
    press_slope = slope(press_padded, local_weights)
    new_stream = jnp.stack([stream[0] + wave_x * press_slab[1], stream[1] - wave_x * press_slab[0]])
    new_span = jnp.stack([span[0] + wave_z * press_slab[1], span[1] - wave_z * press_slab[0]])
    new_normal = normal - press_slope
    return jnp.stack([new_stream, new_normal, new_span])


def unit_waves(place, unit, halves, gap):
    kx = lax.div(unit, halves)
    half = lax.rem(unit, halves)
    wave_x = 0.125 * (place[1] + kx).astype(jnp.float32)
    lane = lax.broadcasted_iota(jnp.int32, (gap, LANES), 1)
    wave_z = 0.05 * (place[2] + half * LANES + lane).astype(jnp.float32)
    return wave_x, wave_z


def shifted(field, before, after):
    rows = field.shape[0]
    row = lax.broadcasted_iota(jnp.int32, field.shape, 0)
    prev = jnp.where(row == 0, before, pltpu.roll(field, 1, 0))
    nxt = jnp.where(row == rows - 1, after, pltpu.roll(field, rows - 1, 0))
    return prev, nxt


def pick(shifts, step):
    value = shifts[0]
    for at, shift in enumerate(shifts[1:], 1):
        value = jnp.where(step == at, shift, value)
    return value


def here(groups, chunk, shift):
    return chunk * groups + lax.rem(lax.axis_index("gy") + shift + groups, groups)


def bases(kx_local, span_dev):
    return None, lax.axis_index("gx") * kx_local, lax.axis_index("gz") * span_dev


def divergence_kernel(chunk, groups, halves, sizes, shifts, vel, stencil, *refs):
    outs, (turned, weights) = refs[: len(shifts)], refs[-2:]
    step = pl.program_id(0)
    rows = vel.shape[3]
    unit = here(groups, chunk, pick(shifts, step))
    wave_x, wave_z = unit_waves(bases(*sizes), unit, halves, 1)

    @pl.when(step == 0)
    def _():
        taps = jnp.concatenate(
            [stencil[...], jnp.zeros((LANES - 3, stencil.shape[1]), jnp.float32)], 0
        )
        turned[...] = taps.T
        mine = turned[pl.ds(pl.multiple_of(lax.axis_index("gy") * rows, EDGE), rows), :]
        for tap in range(3):
            weights[tap] = jnp.broadcast_to(mine[:, tap : tap + 1], (rows, LANES))
        if len(refs) > len(shifts) + 2:
            refs[len(shifts)][...] = weights[...]

    def write(out):
        edges = []
        for part, sign in ((0, -1.0), (1, 1.0)):
            normal = vel[1, part, 0]
            prev, nxt = shifted(normal, 0.0, 0.0)
            out[part * rows : (part + 1) * rows, :] = (
                sign * (wave_x * vel[0, 1 - part, 0] + wave_z * vel[2, 1 - part, 0])
                + (weights[0] * prev + weights[1] * normal + weights[2] * nxt)
            )
            edges += [vel[1, part, 0, 0:1, :], vel[1, part, 0, rows - 1 : rows, :]]
        edges.append(jnp.zeros((EDGE - 4, LANES), jnp.float32))
        out[2 * rows :, :] = jnp.concatenate(edges, 0)

    for at in range(len(shifts)):
        pl.when(step == at)(functools.partial(write, outs[at]))


def split_kernel(pieces, *refs):
    sources, (high, low, high_t, low_t), full = refs[:pieces], refs[pieces:-1], refs[-1]
    at = 0
    for source in sources:
        full[at : at + source.shape[0], :] = source[...]
        at += source.shape[0]
    size = full.shape[0]
    for j in range(0, size, LANES):
        block = full[j : j + LANES, :]
        top = block.astype(jnp.bfloat16)
        high[j : j + LANES, :] = top
        low[j : j + LANES, :] = (block - top.astype(jnp.float32)).astype(jnp.bfloat16)
        block = full[:, j : j + LANES].T
        top = block.astype(jnp.bfloat16)
        high_t[j : j + LANES, :] = top
        low_t[j : j + LANES, :] = (block - top.astype(jnp.float32)).astype(jnp.bfloat16)


def three_products(high, low, values):
    top = values.astype(jnp.bfloat16)
    rest = (values - top.astype(jnp.float32)).astype(jnp.bfloat16)
    dot = functools.partial(jnp.dot, preferred_element_type=jnp.float32)
    return dot(high[...], top) + (dot(high[...], rest) + dot(low[...], top))


def solve_kernel(chunk, groups, halves, sizes, stencil, rates, high, low, high_t, low_t, *refs):
    blocks, outs = refs[:groups], refs[groups : 2 * groups]
    field, edge = refs[2 * groups :]
    rows = (blocks[0].shape[0] - EDGE) // 2
    rows_all = high.shape[0]
    me = lax.axis_index("gy")
    for k in range(groups):
        source = lax.rem(me - k + groups, groups)
        base = pl.multiple_of(source * rows + EDGE, EDGE)
        for part in range(2):
            field[pl.ds(base, rows), part * LANES : (part + 1) * LANES] = blocks[k][
                part * rows : (part + 1) * rows, :
            ]
        edge[source] = blocks[k][2 * rows :, :]
    for s in range(groups - 1):
        cut = (s + 1) * rows
        for part in range(2):
            lanes = slice(part * LANES, (part + 1) * LANES)
            above = edge[s + 1, 2 * part : 2 * part + 1, :]
            below = edge[s, 2 * part + 1 : 2 * part + 2, :]
            field[EDGE + cut - 1 : EDGE + cut, lanes] += stencil[2, cut - 1] * above
            field[EDGE + cut : EDGE + cut + 1, lanes] += stencil[0, cut] * below
    modal = three_products(high, low, field[EDGE : EDGE + rows_all, :])
    wave_x, wave_z = unit_waves(bases(*sizes), chunk * groups + me, halves, 1)
    scale = -1.0 / (rates[...] + wave_x * wave_x + wave_z * wave_z)
    modal = jnp.concatenate([modal[:, :LANES] * scale, modal[:, LANES:] * scale], 1)
    field[EDGE : EDGE + rows_all, :] = three_products(high_t, low_t, modal)
    field[0:EDGE, :] = jnp.zeros((EDGE, 2 * LANES), jnp.float32)
    field[EDGE + rows_all :, :] = jnp.zeros((EDGE, 2 * LANES), jnp.float32)
    for k in range(groups):
        target = lax.rem(me + k, groups)
        start = pl.multiple_of(target * rows, EDGE)
        edges = []
        for part in range(2):
            lanes = slice(part * LANES, (part + 1) * LANES)
            outs[k][part * rows : (part + 1) * rows, :] = field[pl.ds(start + EDGE, rows), lanes]
            edges.append(field[pl.ds(start, EDGE), lanes][EDGE - 1 :, :])
            edges.append(field[pl.ds(start + EDGE + rows, EDGE), lanes][:1, :])
        edges.append(jnp.zeros((EDGE - 4, LANES), jnp.float32))
        outs[k][2 * rows :, :] = jnp.concatenate(edges, 0)


def project_kernel(chunk, groups, halves, sizes, shifts, vel, weights, *refs):
    blocks, out = refs[: len(shifts)], refs[-1]
    step = pl.program_id(0)
    rows = vel.shape[3]
    unit = here(groups, chunk, -pick(shifts, step))
    wave_x, wave_z = unit_waves(bases(*sizes), unit, halves, 1)

    def write(block):
        for part, sign in ((0, 1.0), (1, -1.0)):
            other = block[(1 - part) * rows : (2 - part) * rows, :]
            out[0, part, 0] = vel[0, part, 0] + (sign * wave_x) * other
            out[2, part, 0] = vel[2, part, 0] + (sign * wave_z) * other
            press = block[part * rows : (part + 1) * rows, :]
            at = 2 * rows + 2 * part
            prev, nxt = shifted(press, block[at : at + 1, :], block[at + 1 : at + 2, :])
            out[1, part, 0] = vel[1, part, 0] - (
                weights[0] * prev + weights[1] * press + weights[2] * nxt
            )

    for at in range(len(shifts)):
        pl.when(step == at)(functools.partial(write, blocks[at]))


def shift_order(groups):
    return sorted(range(1, groups), key=lambda k: abs(2 * k - groups))


def gathered_rows(basis, mode_rates):
    gx, gz = lax.axis_size("gx"), lax.axis_size("gz")
    names = ("gx", "gz")
    if (gx, gz) != (4, 2):
        return [lax.all_gather(basis, names, axis=0, tiled=True)], mode_rates

    def swap(value, a, b):
        return lax.ppermute(
            value,
            names,
            [(x * gz + z, (x ^ a) * gz + (z ^ b)) for x in range(gx) for z in range(gz)],
        )

    flips = ((0, 0), (2, 0), (0, 1), (2, 1))
    pieces = [basis] + [swap(basis, *flips[i]) for i in range(1, 4)]
    pieces += [swap(piece, 1, 0) for piece in pieces]
    count = basis.shape[0]
    x, z = lax.axis_index("gx"), lax.axis_index("gz")
    order = [(a + c, b) for c in (0, 1) for a, b in flips]
    rates = jnp.concatenate(
        [
            lax.dynamic_slice_in_dim(mode_rates, ((x ^ a) * gz + (z ^ b)) * count, count, 0)
            for a, b in order
        ]
    )
    return pieces, rates


def fast_device(velocity, stencil, mode_rates, basis):
    rows, kx_local, span_dev = velocity.shape[2:]
    rows_all = stencil.shape[1]
    groups = lax.axis_size("gy")
    halves = span_dev // LANES
    chunks = kx_local * halves // groups
    sizes = (kx_local, span_dev)
    vel = jnp.transpose(velocity, (0, 1, 3, 2, 4))
    block = jax.ShapeDtypeStruct((2 * rows + EDGE, LANES), jnp.float32)
    taps = jax.ShapeDtypeStruct((3, rows, LANES), jnp.float32)
    whole = pl.BlockSpec(memory_space=pltpu.VMEM)
    held = pl.BlockSpec(block.shape, lambda i: (0, 0))
    held_taps = pl.BlockSpec(taps.shape, lambda i: (0, 0, 0))
    unit_bytes = 6 * rows * LANES * 4
    params = pltpu.CompilerParams(vmem_limit_bytes=40 * 2**20)
    wide_params = pltpu.CompilerParams(vmem_limit_bytes=60 * 2**20)
    first = shift_order(groups)

    def unit_spec(chunk, shifts, sign):
        def index(i):
            unit = here(groups, chunk, sign * pick(shifts, i))
            return 0, 0, lax.div(unit, halves), 0, lax.rem(unit, halves)

        return pl.BlockSpec((3, 2, 1, rows, LANES), index)

    def exchange(parts):
        sent = {0: parts[0]}
        for k in shift_order(groups):
            sent[k] = lax.ppermute(parts[k], "gy", [(s, (s + k) % groups) for s in range(groups)])
        return [sent[k] for k in range(groups)]

    def diverge(chunk, shifts, with_taps=False):
        extra = [taps] if with_taps else []
        outs = pl.pallas_call(
            functools.partial(divergence_kernel, chunk, groups, halves, sizes, shifts),
            grid=(len(shifts),),
            in_specs=[unit_spec(chunk, shifts, 1), pl.BlockSpec(stencil.shape, lambda i: (0, 0))],
            out_specs=[held] * len(shifts) + [held_taps] * len(extra),
            out_shape=[block] * len(shifts) + extra,
            scratch_shapes=[
                pltpu.VMEM((rows_all, LANES), jnp.float32),
                pltpu.VMEM(taps.shape, jnp.float32),
            ],
            compiler_params=wide_params,
            name="divergence",
            cost_estimate=pl.CostEstimate(
                flops=len(shifts) * unit_bytes,
                bytes_accessed=2 * len(shifts) * unit_bytes,
                transcendentals=0,
            ),
        )(vel, stencil)
        return dict(zip(shifts, outs)), outs[-1]

    arrived = []
    for chunk in range(chunks):
        if chunk == 0:
            parts, _ = diverge(chunk, first[:1])
            others, weights = diverge(chunk, first[1:] + [0], True)
            parts.update(others)
        else:
            parts, _ = diverge(chunk, first + [0])
        arrived.append(exchange(parts))
    pieces, rates = gathered_rows(basis, mode_rates)
    rates = jnp.broadcast_to(rates[:, None], (rows_all, LANES))
    matrix = jax.ShapeDtypeStruct((rows_all, rows_all), jnp.bfloat16)
    splits = pl.pallas_call(
        functools.partial(split_kernel, len(pieces)),
        in_specs=[whole] * len(pieces),
        out_specs=[whole] * 4,
        out_shape=[matrix] * 4,
        scratch_shapes=[pltpu.VMEM((rows_all, rows_all), jnp.float32)],
        compiler_params=params,
        name="split",
        cost_estimate=pl.CostEstimate(
            flops=4 * rows_all**2, bytes_accessed=12 * rows_all**2, transcendentals=0
        ),
    )(*pieces)

    def solve(chunk, blocks):
        return pl.pallas_call(
            functools.partial(solve_kernel, chunk, groups, halves, sizes),
            in_specs=[pl.BlockSpec(memory_space=pltpu.SMEM)] + [whole] * (5 + groups),
            out_specs=[whole] * groups,
            out_shape=[block] * groups,
            scratch_shapes=[
                pltpu.VMEM((rows_all + 2 * EDGE, 2 * LANES), jnp.float32),
                pltpu.VMEM((groups, EDGE, LANES), jnp.float32),
            ],
            compiler_params=params,
            name="solve",
            cost_estimate=pl.CostEstimate(
                flops=12 * rows_all**2 * 2 * LANES,
                bytes_accessed=8 * rows_all**2 + 8 * block.size * groups,
                transcendentals=0,
            ),
        )(stencil, rates, *splits, *blocks)

    returned = []
    for chunk in range(chunks):
        parts = solve(chunk, arrived[chunk])
        returned.append(exchange(parts))
    out = None
    for chunk in range(chunks):
        steps = [[0] + first]
        if chunk == chunks - 1:
            steps = [[0] + first[:1], first[1:]]
        for shifts in steps:
            carried = [] if out is None else [out]
            call = pl.pallas_call(
                functools.partial(project_kernel, chunk, groups, halves, sizes, shifts),
                grid=(len(shifts),),
                in_specs=[unit_spec(chunk, shifts, -1), held_taps]
                + [held] * len(shifts)
                + [pl.BlockSpec(memory_space=pl.ANY)] * len(carried),
                out_specs=unit_spec(chunk, shifts, -1),
                out_shape=jax.ShapeDtypeStruct(vel.shape, jnp.float32),
                input_output_aliases={2 + len(shifts): 0} if carried else {},
                compiler_params=params,
                name="project",
                cost_estimate=pl.CostEstimate(
                    flops=len(shifts) * unit_bytes,
                    bytes_accessed=3 * len(shifts) * unit_bytes,
                    transcendentals=0,
                ),
            )
            out = call(vel, weights, *[returned[chunk][k] for k in shifts], *carried)
    return jnp.transpose(out, (0, 1, 3, 2, 4))


def fits(shape, rows_all, groups):
    rows, kx_local, span_dev = shape
    units = kx_local * (span_dev // LANES)
    return (
        span_dev % LANES == 0
        and units >= groups
        and units % groups == 0
        and rows % EDGE == 0
        and rows_all % LANES == 0
    )


def per_device(velocity, stencil, mode_rates, basis):
    if not fits(velocity.shape[2:], stencil.shape[1], lax.axis_size("gy")):
        return plain_device(velocity, stencil, mode_rates, basis)
    return fast_device(velocity, stencil, mode_rates, basis)


def solution(mesh):
    placed = (P(None, None, "gy", "gx", "gz"), P(), P(), P(("gx", "gz"), None))
    return jax.shard_map(
        per_device,
        mesh=mesh,
        in_specs=placed,
        out_specs=P(None, None, "gy", "gx", "gz"),
        check_vma=False,
    )
```

```python
import functools

import jax
import jax.numpy as jnp
from jax import lax
from jax.experimental import pallas as pl
from jax.experimental.pallas import tpu as pltpu
from jax.sharding import PartitionSpec as P


LANES = 128
EDGE = 8


def with_halo(cells, sides, width):
    for axis, dim in sides:
        count = lax.axis_size(axis)
        ends = count - 1
        head = lax.slice_in_dim(cells, 0, width, axis=dim)
        tail = lax.slice_in_dim(cells, cells.shape[dim] - width, cells.shape[dim], axis=dim)
        cells = jnp.concatenate(
            [
                lax.ppermute(tail, axis, [(i, (i + 1) % count) for i in range(ends)]),
                cells,
                lax.ppermute(head, axis, [((i + 1) % count, i) for i in range(ends)]),
            ],
            axis=dim,
        )
    return cells


def coefficients(stencil, start, count, trailing):
    rows_part = lax.dynamic_slice_in_dim(stencil, start, count, 1)
    shape = (1, count) + (1,) * trailing
    return (rows_part[0].reshape(shape), rows_part[1].reshape(shape), rows_part[2].reshape(shape))


def slope(padded, weights):
    lower, centre, upper = weights
    return lower * padded[:, :-2] + centre * padded[:, 1:-1] + upper * padded[:, 2:]


def plain_device(velocity, stencil, mode_rates, basis):
    rows_dev = velocity.shape[2]
    kx_local = velocity.shape[3]
    span_dev = velocity.shape[4]
    rows_all = stencil.shape[1]
    groups = lax.axis_size("gy")
    flat_cols = kx_local * span_dev
    pencil_cols = flat_cols // groups
    slab_index = lax.axis_index("gy")
    stream_base = lax.axis_index("gx") * kx_local
    span_base = lax.axis_index("gz") * span_dev
    wave_x = (0.125 * (stream_base + lax.iota(jnp.int32, kx_local)).astype(jnp.float32)).reshape(
        1, kx_local, 1
    )
    wave_z = (0.05 * (span_base + lax.iota(jnp.int32, span_dev)).astype(jnp.float32)).reshape(
        1, 1, span_dev
    )
    column_ids = slab_index * pencil_cols + lax.iota(jnp.int32, pencil_cols)
    wave_px = 0.125 * (stream_base + column_ids // span_dev).astype(jnp.float32)
    wave_pz = 0.05 * (span_base + column_ids % span_dev).astype(jnp.float32)
    local_weights = coefficients(stencil, slab_index * rows_dev, rows_dev, 2)
    full_basis = lax.all_gather(basis, ("gx", "gz"), axis=0, tiled=True)
    stream = velocity[0]
    normal = velocity[1]
    span = velocity[2]
    horizontal = jnp.stack(
        [-(wave_x * stream[1]) - wave_z * span[1], wave_x * stream[0] + wave_z * span[0]]
    )
    padded = with_halo(normal, (("gy", 1),), 1)
    divergence = (horizontal + slope(padded, local_weights)).reshape(2, rows_dev, flat_cols)
    columns = lax.all_to_all(divergence, "gy", split_axis=2, concat_axis=1, tiled=True)
    modal = jnp.einsum("my,ryp->rmp", full_basis, columns, precision=lax.Precision.HIGHEST)
    scale = -1.0 / (
        mode_rates.reshape(rows_all, 1)
        + (wave_px * wave_px + wave_pz * wave_pz).reshape(1, pencil_cols)
    )
    pressure = jnp.einsum(
        "my,rmp->ryp", full_basis, modal * scale[None], precision=lax.Precision.HIGHEST
    )
    press_flat = lax.all_to_all(pressure, "gy", split_axis=1, concat_axis=2, tiled=True)
    press_slab = press_flat.reshape(2, rows_dev, kx_local, span_dev)
    press_padded = with_halo(press_slab, (("gy", 1),), 1)
    press_slope = slope(press_padded, local_weights)
    new_stream = jnp.stack([stream[0] + wave_x * press_slab[1], stream[1] - wave_x * press_slab[0]])
    new_span = jnp.stack([span[0] + wave_z * press_slab[1], span[1] - wave_z * press_slab[0]])
    new_normal = normal - press_slope
    return jnp.stack([new_stream, new_normal, new_span])


def unit_waves(place, unit, halves, gap):
    kx = lax.div(unit, halves)
    half = lax.rem(unit, halves)
    wave_x = 0.125 * (place[1] + kx).astype(jnp.float32)
    lane = lax.broadcasted_iota(jnp.int32, (gap, LANES), 1)
    wave_z = 0.05 * (place[2] + half * LANES + lane).astype(jnp.float32)
    return wave_x, wave_z


def shifted(field, before, after):
    rows = field.shape[0]
    row = lax.broadcasted_iota(jnp.int32, field.shape, 0)
    prev = jnp.where(row == 0, before, pltpu.roll(field, 1, 0))
    nxt = jnp.where(row == rows - 1, after, pltpu.roll(field, rows - 1, 0))
    return prev, nxt


def pick(flips, step):
    value = jnp.int32(flips[0])
    for at, flip in enumerate(flips[1:], 1):
        value = jnp.where(step == at, jnp.int32(flip), value)
    return value


def partner(flip):
    return lax.bitwise_xor(lax.axis_index("gy"), jnp.int32(flip))


def bases(kx_local, span_dev):
    return None, lax.axis_index("gx") * kx_local, lax.axis_index("gz") * span_dev


def divergence_kernel(chunk, groups, halves, sizes, flips, vel, stencil, *refs):
    outs, (turned, weights) = refs[: len(flips)], refs[-2:]
    step = pl.program_id(0)
    rows = vel.shape[3]
    unit = chunk * groups + partner(pick(flips, step))
    wave_x, wave_z = unit_waves(bases(*sizes), unit, halves, 1)

    @pl.when(step == 0)
    def _():
        taps = jnp.concatenate(
            [stencil[...], jnp.zeros((LANES - 3, stencil.shape[1]), jnp.float32)], 0
        )
        turned[...] = taps.T
        mine = turned[pl.ds(pl.multiple_of(lax.axis_index("gy") * rows, EDGE), rows), :]
        for tap in range(3):
            weights[tap] = jnp.broadcast_to(mine[:, tap : tap + 1], (rows, LANES))
        if len(refs) > len(flips) + 2:
            refs[len(flips)][...] = weights[...]

    def write(out):
        edges = []
        for part, sign in ((0, -1.0), (1, 1.0)):
            normal = vel[1, part, 0]
            prev, nxt = shifted(normal, 0.0, 0.0)
            out[part * rows : (part + 1) * rows, :] = (
                sign * (wave_x * vel[0, 1 - part, 0] + wave_z * vel[2, 1 - part, 0])
                + (weights[0] * prev + weights[1] * normal + weights[2] * nxt)
            )
            edges += [vel[1, part, 0, 0:1, :], vel[1, part, 0, rows - 1 : rows, :]]
        edges.append(jnp.zeros((EDGE - 4, LANES), jnp.float32))
        out[2 * rows :, :] = jnp.concatenate(edges, 0)

    for at in range(len(flips)):
        pl.when(step == at)(functools.partial(write, outs[at]))


def split_kernel(pieces, *refs):
    sources, (high, low, high_t, low_t), full = refs[:pieces], refs[pieces:-1], refs[-1]
    at = 0
    for source in sources:
        full[at : at + source.shape[0], :] = source[...]
        at += source.shape[0]
    size = full.shape[0]
    for j in range(0, size, LANES):
        block = full[j : j + LANES, :]
        top = block.astype(jnp.bfloat16)
        high[j : j + LANES, :] = top
        low[j : j + LANES, :] = (block - top.astype(jnp.float32)).astype(jnp.bfloat16)
        block = full[:, j : j + LANES].T
        top = block.astype(jnp.bfloat16)
        high_t[j : j + LANES, :] = top
        low_t[j : j + LANES, :] = (block - top.astype(jnp.float32)).astype(jnp.bfloat16)


def three_products(high, low, values):
    top = values.astype(jnp.bfloat16)
    rest = (values - top.astype(jnp.float32)).astype(jnp.bfloat16)
    dot = functools.partial(jnp.dot, preferred_element_type=jnp.float32)
    return dot(high[...], top) + (dot(high[...], rest) + dot(low[...], top))


def solve_kernel(chunk, groups, halves, sizes, stencil, rates, high, low, high_t, low_t, *refs):
    blocks, outs = refs[:groups], refs[groups : 2 * groups]
    field, edge = refs[2 * groups :]
    rows = (blocks[0].shape[0] - EDGE) // 2
    rows_all = high.shape[0]
    me = lax.axis_index("gy")
    for k in range(groups):
        source = partner(k)
        base = pl.multiple_of(source * rows + EDGE, EDGE)
        for part in range(2):
            field[pl.ds(base, rows), part * LANES : (part + 1) * LANES] = blocks[k][
                part * rows : (part + 1) * rows, :
            ]
        edge[source] = blocks[k][2 * rows :, :]
    for s in range(groups - 1):
        cut = (s + 1) * rows
        for part in range(2):
            lanes = slice(part * LANES, (part + 1) * LANES)
            above = edge[s + 1, 2 * part : 2 * part + 1, :]
            below = edge[s, 2 * part + 1 : 2 * part + 2, :]
            field[EDGE + cut - 1 : EDGE + cut, lanes] += stencil[2, cut - 1] * above
            field[EDGE + cut : EDGE + cut + 1, lanes] += stencil[0, cut] * below
    modal = three_products(high, low, field[EDGE : EDGE + rows_all, :])
    wave_x, wave_z = unit_waves(bases(*sizes), chunk * groups + me, halves, 1)
    scale = -1.0 / (rates[...] + wave_x * wave_x + wave_z * wave_z)
    modal = jnp.concatenate([modal[:, :LANES] * scale, modal[:, LANES:] * scale], 1)
    field[EDGE : EDGE + rows_all, :] = three_products(high_t, low_t, modal)
    field[0:EDGE, :] = jnp.zeros((EDGE, 2 * LANES), jnp.float32)
    field[EDGE + rows_all :, :] = jnp.zeros((EDGE, 2 * LANES), jnp.float32)
    for k in range(groups):
        target = partner(k)
        start = pl.multiple_of(target * rows, EDGE)
        edges = []
        for part in range(2):
            lanes = slice(part * LANES, (part + 1) * LANES)
            outs[k][part * rows : (part + 1) * rows, :] = field[pl.ds(start + EDGE, rows), lanes]
            edges.append(field[pl.ds(start, EDGE), lanes][EDGE - 1 :, :])
            edges.append(field[pl.ds(start + EDGE + rows, EDGE), lanes][:1, :])
        edges.append(jnp.zeros((EDGE - 4, LANES), jnp.float32))
        outs[k][2 * rows :, :] = jnp.concatenate(edges, 0)


def project_kernel(chunk, groups, halves, sizes, flips, vel, weights, *refs):
    blocks, out = refs[: len(flips)], refs[-1]
    step = pl.program_id(0)
    rows = vel.shape[3]
    unit = chunk * groups + partner(pick(flips, step))
    wave_x, wave_z = unit_waves(bases(*sizes), unit, halves, 1)

    def write(block):
        for part, sign in ((0, 1.0), (1, -1.0)):
            other = block[(1 - part) * rows : (2 - part) * rows, :]
            out[0, part, 0] = vel[0, part, 0] + (sign * wave_x) * other
            out[2, part, 0] = vel[2, part, 0] + (sign * wave_z) * other
            press = block[part * rows : (part + 1) * rows, :]
            at = 2 * rows + 2 * part
            prev, nxt = shifted(press, block[at : at + 1, :], block[at + 1 : at + 2, :])
            out[1, part, 0] = vel[1, part, 0] - (
                weights[0] * prev + weights[1] * press + weights[2] * nxt
            )

    for at in range(len(flips)):
        pl.when(step == at)(functools.partial(write, blocks[at]))


def flip_order(groups):
    half = groups // 2
    return [*range(half, groups), *range(1, half)]


def last_order(groups):
    half = groups // 2
    return [half, *range(1, half), *range(half + 1, groups)]


def gathered_rows(basis, mode_rates):
    gx, gz = lax.axis_size("gx"), lax.axis_size("gz")
    names = ("gx", "gz")
    if (gx, gz) != (4, 2):
        return [lax.all_gather(basis, names, axis=0, tiled=True)], mode_rates

    def swap(value, a, b):
        return lax.ppermute(
            value,
            names,
            [(x * gz + z, (x ^ a) * gz + (z ^ b)) for x in range(gx) for z in range(gz)],
        )

    flips = ((0, 0), (2, 0), (0, 1), (2, 1))
    pieces = [basis] + [swap(basis, *flips[i]) for i in range(1, 4)]
    pieces += [swap(piece, 1, 0) for piece in pieces]
    count = basis.shape[0]
    x, z = lax.axis_index("gx"), lax.axis_index("gz")
    order = [(a + c, b) for c in (0, 1) for a, b in flips]
    rates = jnp.concatenate(
        [
            lax.dynamic_slice_in_dim(mode_rates, ((x ^ a) * gz + (z ^ b)) * count, count, 0)
            for a, b in order
        ]
    )
    return pieces, rates


def fast_device(velocity, stencil, mode_rates, basis):
    rows, kx_local, span_dev = velocity.shape[2:]
    rows_all = stencil.shape[1]
    groups = lax.axis_size("gy")
    halves = span_dev // LANES
    chunks = kx_local * halves // groups
    sizes = (kx_local, span_dev)
    vel = jnp.transpose(velocity, (0, 1, 3, 2, 4))
    block = jax.ShapeDtypeStruct((2 * rows + EDGE, LANES), jnp.float32)
    taps = jax.ShapeDtypeStruct((3, rows, LANES), jnp.float32)
    whole = pl.BlockSpec(memory_space=pltpu.VMEM)
    held = pl.BlockSpec(block.shape, lambda i: (0, 0))
    held_taps = pl.BlockSpec(taps.shape, lambda i: (0, 0, 0))
    unit_bytes = 6 * rows * LANES * 4
    params = pltpu.CompilerParams(vmem_limit_bytes=40 * 2**20)
    wide_params = pltpu.CompilerParams(vmem_limit_bytes=60 * 2**20)
    first, final = flip_order(groups), last_order(groups)

    def unit_spec(chunk, flips):
        def index(i):
            unit = chunk * groups + partner(pick(flips, i))
            return 0, 0, lax.div(unit, halves), 0, lax.rem(unit, halves)

        return pl.BlockSpec((3, 2, 1, rows, LANES), index)

    def exchange(parts, order):
        sent = {0: parts[0]}
        for k in order:
            sent[k] = lax.ppermute(parts[k], "gy", [(s, s ^ k) for s in range(groups)])
        return [sent[k] for k in range(groups)]

    def diverge(chunk, flips, with_taps=False):
        extra = [taps] if with_taps else []
        outs = pl.pallas_call(
            functools.partial(divergence_kernel, chunk, groups, halves, sizes, flips),
            grid=(len(flips),),
            in_specs=[
                unit_spec(chunk, flips),
                pl.BlockSpec(stencil.shape, lambda i: (0, 0)),
            ],
            out_specs=[held] * len(flips) + [held_taps] * len(extra),
            out_shape=[block] * len(flips) + extra,
            scratch_shapes=[
                pltpu.VMEM((rows_all, LANES), jnp.float32),
                pltpu.VMEM(taps.shape, jnp.float32),
            ],
            compiler_params=wide_params,
            name="divergence",
            cost_estimate=pl.CostEstimate(
                flops=len(flips) * unit_bytes,
                bytes_accessed=2 * len(flips) * unit_bytes,
                transcendentals=0,
            ),
        )(vel, stencil)
        return dict(zip(flips, outs)), outs[-1]

    arrived = []
    for chunk in range(chunks):
        if chunk == 0:
            parts, _ = diverge(chunk, first[:1])
            others, weights = diverge(chunk, first[1:] + [0], True)
            parts.update(others)
        else:
            parts, _ = diverge(chunk, first + [0])
        arrived.append(exchange(parts, first))
    pieces, rates = gathered_rows(basis, mode_rates)
    rates = jnp.broadcast_to(rates[:, None], (rows_all, LANES))
    matrix = jax.ShapeDtypeStruct((rows_all, rows_all), jnp.bfloat16)
    splits = pl.pallas_call(
        functools.partial(split_kernel, len(pieces)),
        in_specs=[whole] * len(pieces),
        out_specs=[whole] * 4,
        out_shape=[matrix] * 4,
        scratch_shapes=[pltpu.VMEM((rows_all, rows_all), jnp.float32)],
        compiler_params=params,
        name="split",
        cost_estimate=pl.CostEstimate(
            flops=4 * rows_all**2, bytes_accessed=12 * rows_all**2, transcendentals=0
        ),
    )(*pieces)

    def solve(chunk, blocks):
        return pl.pallas_call(
            functools.partial(solve_kernel, chunk, groups, halves, sizes),
            in_specs=[pl.BlockSpec(memory_space=pltpu.SMEM)] + [whole] * (5 + groups),
            out_specs=[whole] * groups,
            out_shape=[block] * groups,
            scratch_shapes=[
                pltpu.VMEM((rows_all + 2 * EDGE, 2 * LANES), jnp.float32),
                pltpu.VMEM((groups, EDGE, LANES), jnp.float32),
            ],
            compiler_params=params,
            name="solve",
            cost_estimate=pl.CostEstimate(
                flops=12 * rows_all**2 * 2 * LANES,
                bytes_accessed=8 * rows_all**2 + 8 * block.size * groups,
                transcendentals=0,
            ),
        )(stencil, rates, *splits, *blocks)

    returned = []
    for chunk in range(chunks):
        parts = solve(chunk, arrived[chunk])
        returned.append(exchange(parts, final if chunk == chunks - 1 else first))
    out = None
    for chunk in range(chunks):
        steps = [[0] + first]
        if chunk == chunks - 1:
            steps = [[0] + final[:1], final[1:-1], final[-1:]]
        for flips in filter(None, steps):
            carried = [] if out is None else [out]
            call = pl.pallas_call(
                functools.partial(project_kernel, chunk, groups, halves, sizes, flips),
                grid=(len(flips),),
                in_specs=[unit_spec(chunk, flips), held_taps]
                + [held] * len(flips)
                + [pl.BlockSpec(memory_space=pl.ANY)] * len(carried),
                out_specs=unit_spec(chunk, flips),
                out_shape=jax.ShapeDtypeStruct(vel.shape, jnp.float32),
                input_output_aliases={2 + len(flips): 0} if carried else {},
                compiler_params=params,
                name="project",
                cost_estimate=pl.CostEstimate(
                    flops=len(flips) * unit_bytes,
                    bytes_accessed=3 * len(flips) * unit_bytes,
                    transcendentals=0,
                ),
            )
            out = call(vel, weights, *[returned[chunk][k] for k in flips], *carried)
    return jnp.transpose(out, (0, 1, 3, 2, 4))


def fits(shape, rows_all, groups):
    rows, kx_local, span_dev = shape
    units = kx_local * (span_dev // LANES)
    return (
        span_dev % LANES == 0
        and units >= groups
        and units % groups == 0
        and groups > 1
        and groups & (groups - 1) == 0
        and rows % EDGE == 0
        and rows_all % LANES == 0
    )


def per_device(velocity, stencil, mode_rates, basis):
    if not fits(velocity.shape[2:], stencil.shape[1], lax.axis_size("gy")):
        return plain_device(velocity, stencil, mode_rates, basis)
    return fast_device(velocity, stencil, mode_rates, basis)


def solution(mesh):
    placed = (P(None, None, "gy", "gx", "gz"), P(), P(), P(("gx", "gz"), None))
    return jax.shard_map(
        per_device,
        mesh=mesh,
        in_specs=placed,
        out_specs=P(None, None, "gy", "gx", "gz"),
        check_vma=False,
    )
```

```python
import functools

import jax
import jax.numpy as jnp
from jax import lax
from jax.experimental import pallas as pl
from jax.experimental.pallas import tpu as pltpu
from jax.sharding import PartitionSpec as P


LANES = 128
EDGE = 8


def with_halo(cells, sides, width):
    for axis, dim in sides:
        count = lax.axis_size(axis)
        ends = count - 1
        head = lax.slice_in_dim(cells, 0, width, axis=dim)
        tail = lax.slice_in_dim(cells, cells.shape[dim] - width, cells.shape[dim], axis=dim)
        cells = jnp.concatenate(
            [
                lax.ppermute(tail, axis, [(i, (i + 1) % count) for i in range(ends)]),
                cells,
                lax.ppermute(head, axis, [((i + 1) % count, i) for i in range(ends)]),
            ],
            axis=dim,
        )
    return cells


def coefficients(stencil, start, count, trailing):
    rows_part = lax.dynamic_slice_in_dim(stencil, start, count, 1)
    shape = (1, count) + (1,) * trailing
    return (rows_part[0].reshape(shape), rows_part[1].reshape(shape), rows_part[2].reshape(shape))


def slope(padded, weights):
    lower, centre, upper = weights
    return lower * padded[:, :-2] + centre * padded[:, 1:-1] + upper * padded[:, 2:]


def plain_device(velocity, stencil, mode_rates, basis):
    rows_dev = velocity.shape[2]
    kx_local = velocity.shape[3]
    span_dev = velocity.shape[4]
    rows_all = stencil.shape[1]
    groups = lax.axis_size("gy")
    flat_cols = kx_local * span_dev
    pencil_cols = flat_cols // groups
    slab_index = lax.axis_index("gy")
    stream_base = lax.axis_index("gx") * kx_local
    span_base = lax.axis_index("gz") * span_dev
    wave_x = (0.125 * (stream_base + lax.iota(jnp.int32, kx_local)).astype(jnp.float32)).reshape(
        1, kx_local, 1
    )
    wave_z = (0.05 * (span_base + lax.iota(jnp.int32, span_dev)).astype(jnp.float32)).reshape(
        1, 1, span_dev
    )
    column_ids = slab_index * pencil_cols + lax.iota(jnp.int32, pencil_cols)
    wave_px = 0.125 * (stream_base + column_ids // span_dev).astype(jnp.float32)
    wave_pz = 0.05 * (span_base + column_ids % span_dev).astype(jnp.float32)
    local_weights = coefficients(stencil, slab_index * rows_dev, rows_dev, 2)
    full_basis = lax.all_gather(basis, ("gx", "gz"), axis=0, tiled=True)
    stream = velocity[0]
    normal = velocity[1]
    span = velocity[2]
    horizontal = jnp.stack(
        [-(wave_x * stream[1]) - wave_z * span[1], wave_x * stream[0] + wave_z * span[0]]
    )
    padded = with_halo(normal, (("gy", 1),), 1)
    divergence = (horizontal + slope(padded, local_weights)).reshape(2, rows_dev, flat_cols)
    columns = lax.all_to_all(divergence, "gy", split_axis=2, concat_axis=1, tiled=True)
    modal = jnp.einsum("my,ryp->rmp", full_basis, columns, precision=lax.Precision.HIGHEST)
    scale = -1.0 / (
        mode_rates.reshape(rows_all, 1)
        + (wave_px * wave_px + wave_pz * wave_pz).reshape(1, pencil_cols)
    )
    pressure = jnp.einsum(
        "my,rmp->ryp", full_basis, modal * scale[None], precision=lax.Precision.HIGHEST
    )
    press_flat = lax.all_to_all(pressure, "gy", split_axis=1, concat_axis=2, tiled=True)
    press_slab = press_flat.reshape(2, rows_dev, kx_local, span_dev)
    press_padded = with_halo(press_slab, (("gy", 1),), 1)
    press_slope = slope(press_padded, local_weights)
    new_stream = jnp.stack([stream[0] + wave_x * press_slab[1], stream[1] - wave_x * press_slab[0]])
    new_span = jnp.stack([span[0] + wave_z * press_slab[1], span[1] - wave_z * press_slab[0]])
    new_normal = normal - press_slope
    return jnp.stack([new_stream, new_normal, new_span])


def unit_waves(place, unit, halves, gap):
    kx = lax.div(unit, halves)
    half = lax.rem(unit, halves)
    wave_x = 0.125 * (place[1] + kx).astype(jnp.float32)
    lane = lax.broadcasted_iota(jnp.int32, (gap, LANES), 1)
    wave_z = 0.05 * (place[2] + half * LANES + lane).astype(jnp.float32)
    return wave_x, wave_z


def shifted(field, before, after):
    rows = field.shape[0]
    row = lax.broadcasted_iota(jnp.int32, field.shape, 0)
    prev = jnp.where(row == 0, before, pltpu.roll(field, 1, 0))
    nxt = jnp.where(row == rows - 1, after, pltpu.roll(field, rows - 1, 0))
    return prev, nxt


def pick(flips, step):
    value = jnp.int32(flips[0])
    for at, flip in enumerate(flips[1:], 1):
        value = jnp.where(step == at, jnp.int32(flip), value)
    return value


def partner(flip):
    return lax.bitwise_xor(lax.axis_index("gy"), jnp.int32(flip))


def bases(kx_local, span_dev):
    return None, lax.axis_index("gx") * kx_local, lax.axis_index("gz") * span_dev


def make_weights(stencil, turned, weights):
    rows = weights.shape[1]
    taps = jnp.concatenate(
        [stencil[...], jnp.zeros((LANES - 3, stencil.shape[1]), jnp.float32)], 0
    )
    turned[...] = taps.T
    mine = turned[pl.ds(pl.multiple_of(lax.axis_index("gy") * rows, EDGE), rows), :]
    for tap in range(3):
        weights[tap] = jnp.broadcast_to(mine[:, tap : tap + 1], (rows, LANES))


def write_part(out, part, waves, normal, stream, span, weights):
    wave_x, wave_z = waves
    rows = normal.shape[0]
    prev, nxt = shifted(normal, 0.0, 0.0)
    out[part * rows : (part + 1) * rows, :] = (-1.0, 1.0)[part] * (
        wave_x * stream + wave_z * span
    ) + (weights[0] * prev + weights[1] * normal + weights[2] * nxt)
    return [normal[0:1, :], normal[rows - 1 :, :]]


def write_edges(out, edges):
    edges.append(jnp.zeros((EDGE - len(edges), LANES), jnp.float32))
    out[out.shape[0] - EDGE :, :] = jnp.concatenate(edges, 0)


def first_kernel(halves, sizes, flip, vel, stencil, out, turned, weights, held, sems):
    unit = partner(flip)
    kx, half = lax.div(unit, halves), lax.rem(unit, halves)
    lanes = pl.ds(pl.multiple_of(half * LANES, LANES), LANES)
    copies = {}
    for part in range(2):
        for kind in range(3):
            side = part if kind == 1 else 1 - part
            copies[part, kind] = pltpu.make_async_copy(
                vel.at[kind, side, kx, :, lanes], held.at[kind, side], sems.at[part, kind]
            )
            copies[part, kind].start()
    make_weights(stencil, turned, weights)
    waves = unit_waves(bases(*sizes), unit, halves, 1)
    edges = []
    for part in range(2):
        for kind in range(3):
            copies[part, kind].wait()
        edges += write_part(
            out, part, waves, held[1, part], held[0, 1 - part], held[2, 1 - part], weights
        )
    write_edges(out, edges)


def divergence_kernel(chunk, groups, halves, sizes, flips, vel, stencil, *refs):
    outs, (turned, weights) = refs[: len(flips)], refs[-2:]
    step = pl.program_id(0)
    unit = chunk * groups + partner(pick(flips, step))
    waves = unit_waves(bases(*sizes), unit, halves, 1)

    @pl.when(step == 0)
    def _():
        make_weights(stencil, turned, weights)
        if len(refs) > len(flips) + 2:
            refs[len(flips)][...] = weights[...]

    def write(out):
        edges = []
        for part in range(2):
            edges += write_part(
                out,
                part,
                waves,
                vel[1, part, 0],
                vel[0, 1 - part, 0],
                vel[2, 1 - part, 0],
                weights,
            )
        write_edges(out, edges)

    for at in range(len(flips)):
        pl.when(step == at)(functools.partial(write, outs[at]))


def split_kernel(pieces, *refs):
    sources, (high, low, high_t, low_t), full = refs[:pieces], refs[pieces:-1], refs[-1]
    at = 0
    for source in sources:
        full[at : at + source.shape[0], :] = source[...]
        at += source.shape[0]
    size = full.shape[0]
    for j in range(0, size, LANES):
        block = full[j : j + LANES, :]
        top = block.astype(jnp.bfloat16)
        high[j : j + LANES, :] = top
        low[j : j + LANES, :] = (block - top.astype(jnp.float32)).astype(jnp.bfloat16)
        block = full[:, j : j + LANES].T
        top = block.astype(jnp.bfloat16)
        high_t[j : j + LANES, :] = top
        low_t[j : j + LANES, :] = (block - top.astype(jnp.float32)).astype(jnp.bfloat16)


def three_products(high, low, values):
    top = values.astype(jnp.bfloat16)
    rest = (values - top.astype(jnp.float32)).astype(jnp.bfloat16)
    dot = functools.partial(jnp.dot, preferred_element_type=jnp.float32)
    return dot(high[...], top) + (dot(high[...], rest) + dot(low[...], top))


def solve_kernel(chunk, groups, halves, sizes, stencil, rates, high, low, high_t, low_t, *refs):
    blocks, outs = refs[:groups], refs[groups : 2 * groups]
    field, edge = refs[2 * groups :]
    rows = (blocks[0].shape[0] - EDGE) // 2
    rows_all = high.shape[0]
    me = lax.axis_index("gy")
    for k in range(groups):
        source = partner(k)
        base = pl.multiple_of(source * rows + EDGE, EDGE)
        for part in range(2):
            field[pl.ds(base, rows), part * LANES : (part + 1) * LANES] = blocks[k][
                part * rows : (part + 1) * rows, :
            ]
        edge[source] = blocks[k][2 * rows :, :]
    for s in range(groups - 1):
        cut = (s + 1) * rows
        for part in range(2):
            lanes = slice(part * LANES, (part + 1) * LANES)
            above = edge[s + 1, 2 * part : 2 * part + 1, :]
            below = edge[s, 2 * part + 1 : 2 * part + 2, :]
            field[EDGE + cut - 1 : EDGE + cut, lanes] += stencil[2, cut - 1] * above
            field[EDGE + cut : EDGE + cut + 1, lanes] += stencil[0, cut] * below
    modal = three_products(high, low, field[EDGE : EDGE + rows_all, :])
    wave_x, wave_z = unit_waves(bases(*sizes), chunk * groups + me, halves, 1)
    scale = -1.0 / (rates[...] + wave_x * wave_x + wave_z * wave_z)
    modal = jnp.concatenate([modal[:, :LANES] * scale, modal[:, LANES:] * scale], 1)
    field[EDGE : EDGE + rows_all, :] = three_products(high_t, low_t, modal)
    field[0:EDGE, :] = jnp.zeros((EDGE, 2 * LANES), jnp.float32)
    field[EDGE + rows_all :, :] = jnp.zeros((EDGE, 2 * LANES), jnp.float32)
    for k in range(groups):
        target = partner(k)
        start = pl.multiple_of(target * rows, EDGE)
        edges = []
        for part in range(2):
            lanes = slice(part * LANES, (part + 1) * LANES)
            outs[k][part * rows : (part + 1) * rows, :] = field[pl.ds(start + EDGE, rows), lanes]
            edges.append(field[pl.ds(start, EDGE), lanes][EDGE - 1 :, :])
            edges.append(field[pl.ds(start + EDGE + rows, EDGE), lanes][:1, :])
        edges.append(jnp.zeros((EDGE - 4, LANES), jnp.float32))
        outs[k][2 * rows :, :] = jnp.concatenate(edges, 0)


def project_kernel(chunk, groups, halves, sizes, flips, vel, weights, *refs):
    blocks, out = refs[: len(flips)], refs[-1]
    step = pl.program_id(0)
    rows = vel.shape[3]
    unit = chunk * groups + partner(pick(flips, step))
    wave_x, wave_z = unit_waves(bases(*sizes), unit, halves, 1)

    def write(block):
        for part, sign in ((0, 1.0), (1, -1.0)):
            other = block[(1 - part) * rows : (2 - part) * rows, :]
            out[0, part, 0] = vel[0, part, 0] + (sign * wave_x) * other
            out[2, part, 0] = vel[2, part, 0] + (sign * wave_z) * other
            press = block[part * rows : (part + 1) * rows, :]
            at = 2 * rows + 2 * part
            prev, nxt = shifted(press, block[at : at + 1, :], block[at + 1 : at + 2, :])
            out[1, part, 0] = vel[1, part, 0] - (
                weights[0] * prev + weights[1] * press + weights[2] * nxt
            )

    for at in range(len(flips)):
        pl.when(step == at)(functools.partial(write, blocks[at]))


def flip_order(groups):
    half = groups // 2
    return [*range(half, groups), *range(1, half)]


def last_order(groups):
    half = groups // 2
    return [half, *range(1, half), *range(half + 1, groups)]


def gathered_rows(basis, mode_rates):
    gx, gz = lax.axis_size("gx"), lax.axis_size("gz")
    names = ("gx", "gz")
    if (gx, gz) != (4, 2):
        return [lax.all_gather(basis, names, axis=0, tiled=True)], mode_rates

    def swap(value, a, b):
        return lax.ppermute(
            value,
            names,
            [(x * gz + z, (x ^ a) * gz + (z ^ b)) for x in range(gx) for z in range(gz)],
        )

    flips = ((0, 0), (2, 0), (0, 1), (2, 1))
    pieces = [basis] + [swap(basis, *flips[i]) for i in range(1, 4)]
    pieces += [swap(piece, 1, 0) for piece in pieces]
    count = basis.shape[0]
    x, z = lax.axis_index("gx"), lax.axis_index("gz")
    order = [(a + c, b) for c in (0, 1) for a, b in flips]
    rates = jnp.concatenate(
        [
            lax.dynamic_slice_in_dim(mode_rates, ((x ^ a) * gz + (z ^ b)) * count, count, 0)
            for a, b in order
        ]
    )
    return pieces, rates


def fast_device(velocity, stencil, mode_rates, basis):
    rows, kx_local, span_dev = velocity.shape[2:]
    rows_all = stencil.shape[1]
    groups = lax.axis_size("gy")
    halves = span_dev // LANES
    chunks = kx_local * halves // groups
    sizes = (kx_local, span_dev)
    vel = jnp.transpose(velocity, (0, 1, 3, 2, 4))
    block = jax.ShapeDtypeStruct((2 * rows + EDGE, LANES), jnp.float32)
    taps = jax.ShapeDtypeStruct((3, rows, LANES), jnp.float32)
    whole = pl.BlockSpec(memory_space=pltpu.VMEM)
    held = pl.BlockSpec(block.shape, lambda i: (0, 0))
    held_taps = pl.BlockSpec(taps.shape, lambda i: (0, 0, 0))
    unit_bytes = 6 * rows * LANES * 4
    params = pltpu.CompilerParams(vmem_limit_bytes=40 * 2**20)
    wide_params = pltpu.CompilerParams(vmem_limit_bytes=60 * 2**20)
    first, final = flip_order(groups), last_order(groups)

    def unit_spec(chunk, flips):
        def index(i):
            unit = chunk * groups + partner(pick(flips, i))
            return 0, 0, lax.div(unit, halves), 0, lax.rem(unit, halves)

        return pl.BlockSpec((3, 2, 1, rows, LANES), index)

    def exchange(parts, order):
        sent = {0: parts[0]}
        for k in order:
            sent[k] = lax.ppermute(parts[k], "gy", [(s, s ^ k) for s in range(groups)])
        return [sent[k] for k in range(groups)]

    def diverge(chunk, flips, with_taps=False):
        extra = [taps] if with_taps else []
        outs = pl.pallas_call(
            functools.partial(divergence_kernel, chunk, groups, halves, sizes, flips),
            grid=(len(flips),),
            in_specs=[
                unit_spec(chunk, flips),
                pl.BlockSpec(stencil.shape, lambda i: (0, 0)),
            ],
            out_specs=[held] * len(flips) + [held_taps] * len(extra),
            out_shape=[block] * len(flips) + extra,
            scratch_shapes=[
                pltpu.VMEM((rows_all, LANES), jnp.float32),
                pltpu.VMEM(taps.shape, jnp.float32),
            ],
            compiler_params=wide_params,
            name="divergence",
            cost_estimate=pl.CostEstimate(
                flops=len(flips) * unit_bytes,
                bytes_accessed=2 * len(flips) * unit_bytes,
                transcendentals=0,
            ),
        )(vel, stencil)
        return dict(zip(flips, outs)), outs[-1]

    def begin(flip):
        return pl.pallas_call(
            functools.partial(first_kernel, halves, sizes, flip),
            in_specs=[pl.BlockSpec(memory_space=pl.ANY), whole],
            out_specs=whole,
            out_shape=block,
            scratch_shapes=[
                pltpu.VMEM((rows_all, LANES), jnp.float32),
                pltpu.VMEM(taps.shape, jnp.float32),
                pltpu.VMEM((3, 2, rows, LANES), jnp.float32),
                pltpu.SemaphoreType.DMA((2, 3)),
            ],
            compiler_params=wide_params,
            name="first",
            cost_estimate=pl.CostEstimate(
                flops=unit_bytes, bytes_accessed=2 * unit_bytes, transcendentals=0
            ),
        )(vel, stencil)

    arrived = []
    for chunk in range(chunks):
        if chunk == 0:
            parts = {first[0]: begin(first[0])}
            others, weights = diverge(chunk, first[1:] + [0], True)
            parts.update(others)
        else:
            parts, _ = diverge(chunk, first + [0])
        arrived.append(exchange(parts, first))
    pieces, rates = gathered_rows(basis, mode_rates)
    rates = jnp.broadcast_to(rates[:, None], (rows_all, LANES))
    matrix = jax.ShapeDtypeStruct((rows_all, rows_all), jnp.bfloat16)
    splits = pl.pallas_call(
        functools.partial(split_kernel, len(pieces)),
        in_specs=[whole] * len(pieces),
        out_specs=[whole] * 4,
        out_shape=[matrix] * 4,
        scratch_shapes=[pltpu.VMEM((rows_all, rows_all), jnp.float32)],
        compiler_params=params,
        name="split",
        cost_estimate=pl.CostEstimate(
            flops=4 * rows_all**2, bytes_accessed=12 * rows_all**2, transcendentals=0
        ),
    )(*pieces)

    def solve(chunk, blocks):
        return pl.pallas_call(
            functools.partial(solve_kernel, chunk, groups, halves, sizes),
            in_specs=[pl.BlockSpec(memory_space=pltpu.SMEM)] + [whole] * (5 + groups),
            out_specs=[whole] * groups,
            out_shape=[block] * groups,
            scratch_shapes=[
                pltpu.VMEM((rows_all + 2 * EDGE, 2 * LANES), jnp.float32),
                pltpu.VMEM((groups, EDGE, LANES), jnp.float32),
            ],
            compiler_params=params,
            name="solve",
            cost_estimate=pl.CostEstimate(
                flops=12 * rows_all**2 * 2 * LANES,
                bytes_accessed=8 * rows_all**2 + 8 * block.size * groups,
                transcendentals=0,
            ),
        )(stencil, rates, *splits, *blocks)

    returned = []
    for chunk in range(chunks):
        parts = solve(chunk, arrived[chunk])
        returned.append(exchange(parts, final if chunk == chunks - 1 else first))
    out = None
    steps = [(chunk, [0] + first) for chunk in range(chunks - 1)]
    steps = [(chunks - 1, [0])] + steps + [(chunks - 1, [k]) for k in final]
    for chunk, flips in steps:
        carried = [] if out is None else [out]
        call = pl.pallas_call(
            functools.partial(project_kernel, chunk, groups, halves, sizes, flips),
            grid=(len(flips),),
            in_specs=[unit_spec(chunk, flips), held_taps]
            + [held] * len(flips)
            + [pl.BlockSpec(memory_space=pl.ANY)] * len(carried),
            out_specs=unit_spec(chunk, flips),
            out_shape=jax.ShapeDtypeStruct(vel.shape, jnp.float32),
            input_output_aliases={2 + len(flips): 0} if carried else {},
            compiler_params=params,
            name="project",
            cost_estimate=pl.CostEstimate(
                flops=len(flips) * unit_bytes,
                bytes_accessed=3 * len(flips) * unit_bytes,
                transcendentals=0,
            ),
        )
        out = call(vel, weights, *[returned[chunk][k] for k in flips], *carried)
    return jnp.transpose(out, (0, 1, 3, 2, 4))


def fits(shape, rows_all, groups):
    rows, kx_local, span_dev = shape
    units = kx_local * (span_dev // LANES)
    return (
        span_dev % LANES == 0
        and units >= groups
        and units % groups == 0
        and groups > 1
        and groups & (groups - 1) == 0
        and rows % EDGE == 0
        and rows_all % LANES == 0
    )


def per_device(velocity, stencil, mode_rates, basis):
    if not fits(velocity.shape[2:], stencil.shape[1], lax.axis_size("gy")):
        return plain_device(velocity, stencil, mode_rates, basis)
    return fast_device(velocity, stencil, mode_rates, basis)


def solution(mesh):
    placed = (P(None, None, "gy", "gx", "gz"), P(), P(), P(("gx", "gz"), None))
    return jax.shard_map(
        per_device,
        mesh=mesh,
        in_specs=placed,
        out_specs=P(None, None, "gy", "gx", "gz"),
        check_vma=False,
    )
```
